32 devices in a mesh: group: 2 (over x), row: 16 (over z, y, core).
Axes of the slice: x: 2, y: 2, z: 4, core: 2. Of those that a mesh axis runs over, the one named last changes fastest.
Arguments:
- alignment: bfloat16 [256, 128, 256], P(('group', 'row')), parts along dimension 0, may hold values from -6 to 6
- pair_rep: bfloat16 [256, 128, 128], P(('group', 'row')), parts along dimension 0, may hold values from -6 to 6
- alignment_norm_gain: float32 [256], replicated, may hold values from 0.5 to 1.5
- alignment_norm_offset: float32 [256], replicated, may hold values from -3 to 3
- left_projection_weight: bfloat16 [256, 32], replicated, may hold values from -0.375 to 0.375
- right_projection_weight: bfloat16 [256, 32], replicated, may hold values from -0.375 to 0.375
- outer_weight: bfloat16 [1024, 128], replicated, may hold values from -0.75 to 0.75
- outer_bias: float32 [128], replicated, may hold values from -3 to 3
- pair_gain: float32 [128], replicated, may hold values from 0.5 to 1.5
- pair_shift: float32 [128], replicated, may hold values from -3 to 3
- up_weight: bfloat16 [128, 512], replicated, may hold values from -0.5 to 0.5
- up_bias: float32 [512], replicated, may hold values from -3 to 3
- down_weight: bfloat16 [512, 128], replicated, may hold values from -0.25 to 0.25
- down_bias: float32 [128], replicated, may hold values from -3 to 3
Outputs:
- pair_out: bfloat16 [256, 128, 128], P(('group', 'row')), parts along dimension 0
The draws below stay inside these ranges and needn't reach their ends.
There are 2 independent parts, one for each index of `group`. The reference program is written for one: setup_inputs(seed, part) draws one part's arguments, and reference() takes and returns one part's arrays. A program takes and returns all parts, laid end to end along the dimension named above; an argument that names none is the same for every part. Nothing has to cross between parts.
All inputs are finite; a program needn't handle non-finite values.
Results may differ from the reference program's by a relative error of at most 0.005.
Values may be sent and summed in bfloat16 or wider, within the bound.
No kernel may reach another device: no remote copies, remote signals or barrier semaphores. Data moves between devices by JAX's collectives and lax.ppermute only.
A program may use at most 128 MiB of HBM per device.

```python
import jax
import jax.numpy as jnp
from jax import lax

SEQUENCE_COUNT = 128
ALIGN_CHANNELS = 256
PROJECT_WIDTH = 32
PAIR_W = 128
TRANS = 512
RESIDUE_COUNT = 128


def block_scale(rng, shape, pieces, smallest, high):
    def one(position, parts):
        heights = jax.random.uniform(jax.random.fold_in(jax.random.fold_in(rng, 6), position), (parts,), jnp.float32, smallest / len(pieces), high / len(pieces))
        return jnp.repeat(jnp.exp(heights), shape[position] // parts).reshape((-1,) + (1,) * (len(shape) - position - 1))

    level = one(*pieces[0])
    for cut in pieces[1:]:
        level = level * one(*cut)
    return level


def centred(rng, dims, scale, reach, cuts=(), kind=jnp.bfloat16):
    loudness = block_scale(rng, dims, cuts, -0.22, 0.18) if cuts else 1.0
    values = jax.random.normal(rng, dims, jnp.float32) * scale * loudness
    return jnp.minimum(jnp.maximum(values, -reach), reach).astype(kind)


def setup_inputs(seed: int = 0, part: int = 0) -> dict:
    key_list = jax.random.split(jax.random.key(seed), 15)
    own_keys = jax.random.split(jax.random.fold_in(key_list[14], part), 15)
    return {
        "alignment": centred(own_keys[0], (SEQUENCE_COUNT, RESIDUE_COUNT, ALIGN_CHANNELS), 1.0, 6.0, ((0, 16),)),
        "pair_rep": centred(own_keys[1], (RESIDUE_COUNT, RESIDUE_COUNT, PAIR_W), 1.0, 6.0, ((0, 16),)),
        "alignment_norm_gain": jnp.clip(jax.random.uniform(key_list[2], (ALIGN_CHANNELS,), jnp.float32, 0.5, 1.5), 0.5, 1.5),
        "alignment_norm_offset": centred(key_list[3], (ALIGN_CHANNELS,), 0.5, 3.0, (), jnp.float32),
        "left_projection_weight": centred(key_list[4], (ALIGN_CHANNELS, PROJECT_WIDTH), ALIGN_CHANNELS ** -0.5, 0.375),
        "right_projection_weight": centred(key_list[5], (ALIGN_CHANNELS, PROJECT_WIDTH), ALIGN_CHANNELS ** -0.5, 0.375),
        "outer_weight": centred(key_list[6], (PROJECT_WIDTH * PROJECT_WIDTH, PAIR_W), (2 * PROJECT_WIDTH) ** -0.5, 0.75),
        "outer_bias": centred(key_list[7], (PAIR_W,), 0.5, 3.0, (), jnp.float32),
        "pair_gain": jnp.clip(jax.random.uniform(key_list[8], (PAIR_W,), jnp.float32, 0.5, 1.5), 0.5, 1.5),
        "pair_shift": centred(key_list[9], (PAIR_W,), 0.5, 3.0, (), jnp.float32),
        "up_weight": centred(key_list[10], (PAIR_W, TRANS), PAIR_W ** -0.5, 0.5),
        "up_bias": centred(key_list[11], (TRANS,), 0.5, 3.0, (), jnp.float32),
        "down_weight": centred(key_list[12], (TRANS, PAIR_W), TRANS ** -0.5, 0.25),
        "down_bias": centred(key_list[13], (PAIR_W,), 0.5, 3.0, (), jnp.float32),
    }


epsilon = 1e-05

def layer_norm(values, gain, shift):
    values = values.astype(jnp.float32)
    center = lax.optimization_barrier(jnp.mean(values, axis=-1, keepdims=True))
    spread = lax.optimization_barrier(jnp.mean(jnp.square(values - center), axis=-1, keepdims=True))
    return (values - center) * lax.rsqrt(spread + epsilon) * gain + shift

def pair_update(left_rows, right_rows, pair_tile, layer_params):
    outer_weight, outer_bias, pair_gain, pair_shift, up_weight, up_bias, down_weight, down_bias = layer_params
    rows_i = left_rows.shape[0]
    rows_j = right_rows.shape[0]
    width = outer_weight.shape[1]
    proj_w = left_rows.shape[2]
    seq_total = left_rows.shape[1]
    outer_mean = jnp.einsum('isc,jse->ijce', left_rows.astype(jnp.float32), right_rows.astype(jnp.float32)) * (1.0 / seq_total)
    outer_mean = outer_mean.astype(jnp.bfloat16).reshape(rows_i * rows_j, proj_w * proj_w)
    summed = pair_tile.reshape(rows_i * rows_j, width).astype(jnp.float32) + jnp.dot(outer_mean, outer_weight, preferred_element_type=jnp.float32) + outer_bias
    normed = layer_norm(summed, pair_gain, pair_shift).astype(jnp.bfloat16)
    hidden = jax.nn.relu(jnp.dot(normed, up_weight, preferred_element_type=jnp.float32) + up_bias).astype(jnp.bfloat16)
    result = summed + jnp.dot(hidden, down_weight, preferred_element_type=jnp.float32) + down_bias
    return result.astype(jnp.bfloat16).reshape(rows_i, rows_j, width)

def reference(alignment, pair_rep, alignment_norm_gain, alignment_norm_offset, left_projection_weight, right_projection_weight, outer_weight, outer_bias, pair_gain, pair_shift, up_weight, up_bias, down_weight, down_bias):
    normed = layer_norm(alignment, alignment_norm_gain, alignment_norm_offset).astype(jnp.bfloat16)
    left = jnp.einsum('src,cd->rsd', normed.astype(jnp.float32), left_projection_weight.astype(jnp.float32)).astype(jnp.bfloat16)
    right = jnp.einsum('src,cd->rsd', normed.astype(jnp.float32), right_projection_weight.astype(jnp.float32)).astype(jnp.bfloat16)
    layer_params = (outer_weight, outer_bias, pair_gain, pair_shift, up_weight, up_bias, down_weight, down_bias)
    residues = pair_rep.shape[0]
    block_rows = 16 if residues % 16 == 0 else residues
    block_total = residues // block_rows
    left_blocks = left.reshape(block_total, block_rows, left.shape[1], left.shape[2])
    pair_blocks = pair_rep.reshape(block_total, block_rows, residues, pair_rep.shape[2])

    def one_block(operands):
        return pair_update(operands[0], right, operands[1], layer_params)
    updated = lax.map(one_block, (left_blocks, pair_blocks))
    updated = updated.reshape(residues, residues, pair_rep.shape[2])
    return jnp.transpose(updated, (1, 0, 2))
```

```python
import functools

import jax
import jax.numpy as jnp
from jax import lax
from jax.experimental import pallas as pl
from jax.experimental.pallas import tpu as pltpu
from jax.sharding import PartitionSpec as P

epsilon = 1e-05
LANES = 128
CORES = 2


VMEM = pl.BlockSpec(memory_space=pltpu.VMEM)
SMEM = pl.BlockSpec(memory_space=pltpu.SMEM)


def layer_norm(values, gain, shift):
    values = values.astype(jnp.float32)
    center = jnp.mean(values, axis=-1, keepdims=True)
    spread = jnp.mean(jnp.square(values - center), axis=-1, keepdims=True)
    return (values - center) * lax.rsqrt(spread + epsilon) * gain + shift


def pair_update(left_flat, right_flat, pair_tile, layer_params, proj_w):
    outer_weight, outer_bias, pair_gain, pair_shift, up_weight, up_bias, down_weight, down_bias = (
        layer_params
    )
    rows_i = left_flat.shape[0]
    rows_j = right_flat.shape[0]
    width = outer_weight.shape[1]
    seq_total = left_flat.shape[1] // proj_w
    left_rows = left_flat.reshape(rows_i, seq_total, proj_w)
    right_rows = right_flat.reshape(rows_j, seq_total, proj_w)
    outer_mean = jnp.einsum(
        "isc,jse->ijce", left_rows, right_rows, preferred_element_type=jnp.float32
    ) * (1.0 / seq_total)
    outer_mean = outer_mean.astype(jnp.bfloat16).reshape(rows_i * rows_j, proj_w * proj_w)
    summed = (
        pair_tile.reshape(rows_i * rows_j, width).astype(jnp.float32)
        + jnp.dot(outer_mean, outer_weight, preferred_element_type=jnp.float32)
        + outer_bias
    )
    normed = layer_norm(summed, pair_gain, pair_shift).astype(jnp.bfloat16)
    hidden = jax.nn.relu(
        jnp.dot(normed, up_weight, preferred_element_type=jnp.float32) + up_bias
    ).astype(jnp.bfloat16)
    result = summed + jnp.dot(hidden, down_weight, preferred_element_type=jnp.float32) + down_bias
    return result.astype(jnp.bfloat16).reshape(rows_i, rows_j, width)


def in_blocks(amount, builder):
    if amount > 256 and amount % 256 == 0:
        stacked = lax.map(
            lambda which_k: builder(which_k * 256, 256), jnp.arange(amount // 256, dtype=jnp.int32)
        )
        return stacked.reshape((amount,) + stacked.shape[2:])
    return builder(0, amount)


def plain_shards(alignment, pair_rep, align_gain, align_offset, left_weight, right_weight, *layer_params):
    proj_w = left_weight.shape[1]
    normed = layer_norm(alignment, align_gain, align_offset).astype(jnp.bfloat16)
    both = [
        jnp.einsum("src,cd->rsd", normed, weight, preferred_element_type=jnp.float32).astype(jnp.bfloat16)
        for weight in (left_weight, right_weight)
    ]
    left, right = [
        lax.all_to_all(x, "row", split_axis=0, concat_axis=1, tiled=True).reshape(
            x.shape[0] // lax.axis_size("row"), -1
        )
        for x in both
    ]
    pieces = lax.all_gather(right, "row", axis=0, tiled=True)

    def builder(start, amount):
        segment = lax.dynamic_slice_in_dim(pieces, start, amount, 0)
        pair_tile = lax.dynamic_slice_in_dim(pair_rep, start, amount, 1)
        return jnp.transpose(pair_update(left, segment, pair_tile, layer_params, proj_w), (1, 0, 2))

    columns = in_blocks(pieces.shape[0], builder)
    return lax.all_to_all(columns, "row", split_axis=0, concat_axis=1, tiled=True)


class Layout:
    def __init__(self, seq, residues, own_rows, proj_w):
        self.seq, self.residues, self.rows, self.proj = seq, residues, own_rows, proj_w
        self.fold = LANES // proj_w
        self.chip_rows = CORES * own_rows
        self.pair = self.chip_rows * own_rows
        self.right = self.chip_rows // self.fold * seq
        self.left = proj_w * seq
        self.right_at = self.pair
        self.left_at = self.pair + self.right
        self.total = self.pair + self.right + self.left


def send_kernel(lay, chips, place, x_ref, pair_ref, gain_ref, offset_ref, wl_ref, wr_ref, *rest):
    bufs, (norm_ref, left_ref) = rest[:chips], rest[chips:]
    seq, residues, proj, fold = lay.seq, lay.residues, lay.proj, lay.fold
    f32, bf16 = jnp.float32, jnp.bfloat16
    x = x_ref[...].reshape(seq * residues, x_ref.shape[2])
    normed = layer_norm(x, gain_ref[...], offset_ref[...])
    halves = norm_ref.shape[0]
    for h in range(halves):
        norm_ref[h] = normed[:, h * LANES : (h + 1) * LANES]
    nt = (((1,), (1,)), ((), ()))
    left = lax.dot_general(wl_ref[...], normed.astype(bf16), nt, preferred_element_type=f32)
    for s in range(seq):
        left_ref[s * proj : (s + 1) * proj, :] = left[:, s * residues : (s + 1) * residues]
    per = 16 // seq
    for tile in range(proj // per):
        rows = jnp.concatenate(
            [left_ref[pl.ds(tile * per + b, seq, stride=proj), :] for b in range(per)], axis=0
        ).astype(bf16)
        for buf in bufs:
            buf[lay.left_at + tile * 16 : lay.left_at + (tile + 1) * 16, :] = rows
    groups = residues // fold
    wr = wr_ref[...]
    zero = jnp.zeros_like(wr)
    right = None
    for g in range(fold):
        rows = jnp.concatenate(
            [
                jnp.concatenate(
                    [norm_ref[h, pl.ds(u * fold + g, seq, stride=residues), :] for u in range(groups)], axis=0
                )
                for h in range(halves)
            ],
            axis=1,
        ).astype(bf16)
        weight = jnp.concatenate([wr if h == g else zero for h in range(fold)], axis=0)
        part = lax.dot_general(rows, weight, nt, preferred_element_type=f32)
        right = part if right is None else right + part
    left_ref[...] = right
    for k, buf in enumerate(bufs):
        to = lax.bitwise_xor(place[0], k)
        at = pl.multiple_of(to * lay.right, lay.right)
        buf[lay.right_at : lay.right_at + lay.right, :] = left_ref[pl.ds(at, lay.right), :].astype(bf16)
        at = pl.multiple_of(to * lay.chip_rows, lay.chip_rows)
        tile = pair_ref[:, pl.ds(at, lay.chip_rows), :].astype(f32)
        tile = jnp.swapaxes(tile, 0, 1).reshape(lay.pair, LANES)
        buf[: lay.pair, :] = tile.astype(bf16)


def update_kernel(lay, count, place, *rest):
    bufs = rest[:count]
    (ow_ref, ob_ref, pg_ref, ps_ref, uw_ref, ub_ref, dw_ref, db_ref, out_ref, outer_ref, pair_ref) = rest[count:]
    seq, residues, proj, rows_j, fold = lay.seq, lay.residues, lay.proj, lay.rows, lay.fold
    f32, bf16 = jnp.float32, jnp.bfloat16
    chip, core = place[0], place[1]
    per = 16 // seq
    groups = rows_j // fold
    own = pl.multiple_of(core * (groups * seq), groups * seq)
    spread = []
    for b in range(per):
        rows = []
        for buf in bufs:
            got = buf[pl.ds(lay.right_at + own, groups * seq), :].astype(f32)
            got = jnp.concatenate([got[u * seq : (u + 1) * seq] for u in range(groups)], axis=1)
            zero = jnp.zeros_like(got)
            rows += [got if h == b else zero for h in range(per)]
        spread.append(jnp.concatenate(rows, axis=0).T.astype(bf16))
    right = jnp.concatenate(spread, axis=0)
    wide = 2
    scale = 1.0 / (seq * count)
    for tile in range(0, proj // per, wide):
        left = jnp.concatenate(
            [
                jnp.concatenate([buf[lay.left_at + t * 16 : lay.left_at + (t + 1) * 16, :] for buf in bufs], axis=0)
                for t in range(tile, tile + wide)
            ],
            axis=1,
        )
        x = (jnp.dot(right, left, preferred_element_type=f32) * scale).astype(bf16)
        for b in range(per):
            for w in range(wide):
                c = (tile + w) * per + b
                for j in range(rows_j):
                    at = (b * rows_j + j) * proj
                    outer_ref[c * proj : (c + 1) * proj, j * residues : (j + 1) * residues] = x[
                        at : at + proj, w * residues : (w + 1) * residues
                    ]
    own = pl.multiple_of(core * (rows_j * rows_j), rows_j * rows_j)
    for m, buf in enumerate(bufs):
        sender = lax.bitwise_xor(chip * CORES + core, m)
        got = buf[pl.ds(own, rows_j * rows_j), :].astype(f32)
        for j in range(rows_j):
            pair_ref[j, pl.ds(pl.multiple_of(sender * rows_j, rows_j), rows_j), :] = got[j * rows_j : (j + 1) * rows_j]
    added = lax.dot_general(ow_ref[...], outer_ref[...], (((0,), (0,)), ((), ())), preferred_element_type=f32)
    step = 4
    for j0 in range(0, rows_j, step):
        summed = jnp.concatenate(
            [added[:, j * residues : (j + 1) * residues].T + pair_ref[j] for j in range(j0, j0 + step)], axis=0
        )
        summed = summed + ob_ref[...]
        normed = layer_norm(summed, pg_ref[...], ps_ref[...]).astype(bf16)
        hidden = jnp.dot(normed, uw_ref[...], preferred_element_type=f32) + ub_ref[...]
        hidden = jnp.maximum(hidden, 0.0).astype(bf16)
        result = summed + jnp.dot(hidden, dw_ref[...], preferred_element_type=f32) + db_ref[...]
        out_ref[j0 : j0 + step] = result.astype(bf16).reshape(step, residues, LANES)


def chip_order(chips):
    return sorted(range(1, chips), key=lambda k: (-(k // 4), k))


def fast_shards(n, alignment, pair_rep, align_gain, align_offset, left_weight, right_weight, *layer_params):
    seq, residues, _ = alignment.shape
    lay = Layout(seq, residues, pair_rep.shape[0], left_weight.shape[1])
    chips = n // CORES
    me = lax.axis_index("row")
    place = jnp.stack([me // CORES, me % CORES]).astype(jnp.int32)
    bufs = pl.pallas_call(
        functools.partial(send_kernel, lay, chips),
        out_shape=[jax.ShapeDtypeStruct((lay.total, LANES), jnp.bfloat16)] * chips,
        in_specs=[SMEM] + [VMEM] * 6,
        out_specs=[VMEM] * chips,
        scratch_shapes=[
            pltpu.VMEM((alignment.shape[2] // LANES, seq * residues, LANES), jnp.float32),
            pltpu.VMEM((seq * lay.proj, LANES), jnp.float32),
        ],
        name="send",
    )(
        place,
        alignment,
        pair_rep,
        align_gain.reshape(1, -1),
        align_offset.reshape(1, -1),
        left_weight.T,
        right_weight.T,
    )

    def permute(x, k):
        return lax.ppermute(x, "row", [(d, d ^ k) for d in range(n)])

    got = {0: bufs[0], 1: permute(bufs[0], 1)}
    for k in chip_order(chips):
        got[CORES * k] = permute(bufs[k], CORES * k)
    for k in chip_order(chips):
        got[CORES * k + 1] = permute(got[CORES * k], 1)
    ow, ob, pg, ps, uw, ub, dw, db = layer_params
    rows_j = lay.rows
    return pl.pallas_call(
        functools.partial(update_kernel, lay, n),
        out_shape=jax.ShapeDtypeStruct((rows_j, residues, LANES), jnp.bfloat16),
        in_specs=[SMEM] + [VMEM] * (n + 8),
        out_specs=VMEM,
        scratch_shapes=[
            pltpu.VMEM((lay.proj * lay.proj, rows_j * residues), jnp.bfloat16),
            pltpu.VMEM((rows_j, residues, LANES), jnp.float32),
        ],
        name="update",
    )(
        place,
        *[got[m] for m in range(n)],
        ow,
        ob.reshape(1, -1),
        pg.reshape(1, -1),
        ps.reshape(1, -1),
        uw,
        ub.reshape(1, -1),
        dw,
        db.reshape(1, -1),
    )


def fits(n, alignment, pair_rep, left_weight):
    seq, residues, _ = alignment.shape
    rows, _, width = pair_rep.shape
    return (
        n >= 4
        and n & (n - 1) == 0
        and seq == 8
        and rows == 8
        and residues == LANES
        and width == LANES
        and left_weight.shape[1] == 32
    )


def solution(mesh):
    n = mesh.shape["row"]

    def shards(alignment, pair_rep, align_gain, align_offset, left_weight, right_weight, *layer_params):
        body = plain_shards
        if fits(n, alignment, pair_rep, left_weight):
            body = functools.partial(fast_shards, n)
        return body(alignment, pair_rep, align_gain, align_offset, left_weight, right_weight, *layer_params)

    split = P(("group", "row"), None, None)
    return jax.shard_map(
        shards,
        mesh=mesh,
        in_specs=(split, split) + (P(),) * 12,
        out_specs=split,
        check_vma=False,
    )
```

```python
import functools

import jax
import jax.numpy as jnp
from jax import lax
from jax.experimental import pallas as pl
from jax.experimental.pallas import tpu as pltpu
from jax.sharding import PartitionSpec as P


epsilon = 1e-05
LANES = 128
CORES = 2


VMEM = pl.BlockSpec(memory_space=pltpu.VMEM)
SMEM = pl.BlockSpec(memory_space=pltpu.SMEM)
HBM = pl.BlockSpec(memory_space=pltpu.HBM)


def layer_norm(values, gain, shift):
    values = values.astype(jnp.float32)
    center = jnp.mean(values, axis=-1, keepdims=True)
    spread = jnp.mean(jnp.square(values - center), axis=-1, keepdims=True)
    return (values - center) * lax.rsqrt(spread + epsilon) * gain + shift


def pair_update(left_flat, right_flat, pair_tile, layer_params, proj_w):
    outer_weight, outer_bias, pair_gain, pair_shift, up_weight, up_bias, down_weight, down_bias = (
        layer_params
    )
    rows_i = left_flat.shape[0]
    rows_j = right_flat.shape[0]
    width = outer_weight.shape[1]
    seq_total = left_flat.shape[1] // proj_w
    left_rows = left_flat.reshape(rows_i, seq_total, proj_w)
    right_rows = right_flat.reshape(rows_j, seq_total, proj_w)
    outer_mean = jnp.einsum(
        "isc,jse->ijce", left_rows, right_rows, preferred_element_type=jnp.float32
    ) * (1.0 / seq_total)
    outer_mean = outer_mean.astype(jnp.bfloat16).reshape(rows_i * rows_j, proj_w * proj_w)
    summed = (
        pair_tile.reshape(rows_i * rows_j, width).astype(jnp.float32)
        + jnp.dot(outer_mean, outer_weight, preferred_element_type=jnp.float32)
        + outer_bias
    )
    normed = layer_norm(summed, pair_gain, pair_shift).astype(jnp.bfloat16)
    hidden = jax.nn.relu(
        jnp.dot(normed, up_weight, preferred_element_type=jnp.float32) + up_bias
    ).astype(jnp.bfloat16)
    result = summed + jnp.dot(hidden, down_weight, preferred_element_type=jnp.float32) + down_bias
    return result.astype(jnp.bfloat16).reshape(rows_i, rows_j, width)


def in_blocks(amount, builder):
    if amount > 256 and amount % 256 == 0:
        stacked = lax.map(
            lambda which_k: builder(which_k * 256, 256), jnp.arange(amount // 256, dtype=jnp.int32)
        )
        return stacked.reshape((amount,) + stacked.shape[2:])
    return builder(0, amount)


def plain_shards(alignment, pair_rep, align_gain, align_offset, left_weight, right_weight, *layer_params):
    proj_w = left_weight.shape[1]
    normed = layer_norm(alignment, align_gain, align_offset).astype(jnp.bfloat16)
    both = [
        jnp.einsum("src,cd->rsd", normed, weight, preferred_element_type=jnp.float32).astype(jnp.bfloat16)
        for weight in (left_weight, right_weight)
    ]
    left, right = [
        lax.all_to_all(x, "row", split_axis=0, concat_axis=1, tiled=True).reshape(
            x.shape[0] // lax.axis_size("row"), -1
        )
        for x in both
    ]
    pieces = lax.all_gather(right, "row", axis=0, tiled=True)

    def builder(start, amount):
        segment = lax.dynamic_slice_in_dim(pieces, start, amount, 0)
        pair_tile = lax.dynamic_slice_in_dim(pair_rep, start, amount, 1)
        return jnp.transpose(pair_update(left, segment, pair_tile, layer_params, proj_w), (1, 0, 2))

    columns = in_blocks(pieces.shape[0], builder)
    return lax.all_to_all(columns, "row", split_axis=0, concat_axis=1, tiled=True)


class Layout:
    def __init__(self, n, seq, residues, own_rows, proj_w):
        self.n, self.chips = n, n // CORES
        self.far = self.chips // 2
        self.seq, self.residues, self.rows, self.proj = seq, residues, own_rows, proj_w
        self.per = 16 // seq
        self.fold = LANES // proj_w
        self.chip_rows = CORES * own_rows
        self.left = proj_w * seq
        self.right = self.chip_rows // self.fold * seq
        self.pair = self.chip_rows * own_rows
        self.relayed = self.left + self.right

    def crosses(self, k):
        return k >= self.far and k % 2 == 0

    def right_at(self, k):
        return self.left + (self.right if self.crosses(k) else 0)

    def pair_at(self, k):
        return 0 if self.pair_only(k) else self.right_at(k) + self.right

    def pair_only(self, k):
        return k >= self.far and k % 2 == 1

    def total(self, k):
        return self.pair_at(k) + self.pair


def send_kernel(lay, place, x_ref, pair_ref, gain_ref, offset_ref, wl_ref, wr_ref, *rest):
    bufs, (norm_ref, left_ref) = rest[: lay.chips], rest[lay.chips :]
    seq, residues, proj, fold = lay.seq, lay.residues, lay.proj, lay.fold
    f32, bf16 = jnp.float32, jnp.bfloat16
    halves = norm_ref.shape[0]
    nt = (((1,), (1,)), ((), ()))
    x = x_ref[...].reshape(seq * residues, x_ref.shape[2])
    normed = layer_norm(x, gain_ref[...], offset_ref[...])
    for h in range(halves):
        norm_ref[h] = normed[:, h * LANES : (h + 1) * LANES]
    left = lax.dot_general(wl_ref[...], normed.astype(bf16), nt, preferred_element_type=f32)
    for s in range(seq):
        left_ref[s * proj : (s + 1) * proj, :] = left[:, s * residues : (s + 1) * residues]
    for tile in range(proj // lay.per):
        rows = jnp.concatenate(
            [left_ref[pl.ds(tile * lay.per + b, seq, stride=proj), :] for b in range(lay.per)], axis=0
        ).astype(bf16)
        for k, buf in enumerate(bufs):
            if not lay.pair_only(k):
                buf[tile * 16 : (tile + 1) * 16, :] = rows
    groups = residues // fold
    wr = wr_ref[...]
    zero = jnp.zeros_like(wr)
    right = None
    for g in range(fold):
        rows = jnp.concatenate(
            [
                jnp.concatenate(
                    [norm_ref[h, pl.ds(u * fold + g, seq, stride=residues), :] for u in range(groups)], axis=0
                )
                for h in range(halves)
            ],
            axis=1,
        ).astype(bf16)
        weight = jnp.concatenate([wr if h == g else zero for h in range(fold)], axis=0)
        part = lax.dot_general(rows, weight, nt, preferred_element_type=f32)
        right = part if right is None else right + part
    left_ref[...] = right

    def right_of(k):
        at = pl.multiple_of(lax.bitwise_xor(place[0], k) * lay.right, lay.right)
        return left_ref[pl.ds(at, lay.right), :].astype(bf16)

    for k, buf in enumerate(bufs):
        if not lay.pair_only(k):
            at = lay.right_at(k)
            buf[at : at + lay.right, :] = right_of(k)
        if lay.crosses(k):
            buf[lay.left : lay.left + lay.right, :] = right_of(k ^ 1)
        at = pl.multiple_of(lax.bitwise_xor(place[0], k) * lay.chip_rows, lay.chip_rows)
        tile = pair_ref[:, pl.ds(at, lay.chip_rows), :].astype(f32)
        tile = jnp.swapaxes(tile, 0, 1).reshape(lay.pair, LANES)
        at = lay.pair_at(k)
        buf[at : at + lay.pair, :] = tile.astype(bf16)


def update_kernel(lay, outers, pairs, place, *rest):
    count = max([b for b, _ in outers] + [b for b, _, _ in pairs]) + 1
    bufs = rest[:count]
    (ow_ref, ob_ref, pg_ref, ps_ref, uw_ref, ub_ref, dw_ref, db_ref, out_ref, outer_ref, pair_ref) = rest[count:]
    seq, residues, proj, rows_j, fold, per = lay.seq, lay.residues, lay.proj, lay.rows, lay.fold, lay.per
    f32, bf16 = jnp.float32, jnp.bfloat16
    chip, core = place[0], place[1]
    groups = rows_j // fold
    own = pl.multiple_of(core * (groups * seq), groups * seq)
    spread = []
    for b in range(per):
        rows = []
        for m, at in outers:
            got = bufs[m][pl.ds(at + own, groups * seq), :].astype(f32)
            got = jnp.concatenate([got[u * seq : (u + 1) * seq] for u in range(groups)], axis=1)
            zero = jnp.zeros_like(got)
            rows += [got if h == b else zero for h in range(per)]
        spread.append(jnp.concatenate(rows, axis=0).T.astype(bf16))
    right = jnp.concatenate(spread, axis=0)
    wide = 2
    scale = 1.0 / (seq * lay.n)
    for tile in range(0, proj // per, wide):
        left = jnp.concatenate(
            [
                jnp.concatenate([bufs[m][t * 16 : (t + 1) * 16, :] for m, _ in outers], axis=0)
                for t in range(tile, tile + wide)
            ],
            axis=1,
        )
        x = (jnp.dot(right, left, preferred_element_type=f32) * scale).astype(bf16)
        for b in range(per):
            for w in range(wide):
                c = (tile + w) * per + b
                for j in range(rows_j):
                    at = (b * rows_j + j) * proj
                    outer_ref[c * proj : (c + 1) * proj, j * residues : (j + 1) * residues] = x[
                        at : at + proj, w * residues : (w + 1) * residues
                    ]
    own = pl.multiple_of(core * (rows_j * rows_j), rows_j * rows_j)
    for m, at, k in pairs:
        sender = lax.bitwise_xor(chip * CORES + core, k)
        got = bufs[m][pl.ds(at + own, rows_j * rows_j), :].astype(f32)
        for j in range(rows_j):
            pair_ref[j, pl.ds(pl.multiple_of(sender * rows_j, rows_j), rows_j), :] = got[j * rows_j : (j + 1) * rows_j]
    added = lax.dot_general(ow_ref[...], outer_ref[...], (((0,), (0,)), ((), ())), preferred_element_type=f32)
    step = 4
    for j0 in range(0, rows_j, step):
        summed = jnp.concatenate(
            [added[:, j * residues : (j + 1) * residues].T + pair_ref[j] for j in range(j0, j0 + step)], axis=0
        )
        summed = summed + ob_ref[...]
        normed = layer_norm(summed, pg_ref[...], ps_ref[...]).astype(bf16)
        hidden = jnp.dot(normed, uw_ref[...], preferred_element_type=f32) + ub_ref[...]
        hidden = jnp.maximum(hidden, 0.0).astype(bf16)
        result = summed + jnp.dot(hidden, dw_ref[...], preferred_element_type=f32) + db_ref[...]
        out_ref[j0 : j0 + step] = result.astype(bf16).reshape(step, residues, LANES)


MIB = 1 << 20
VMEM_BYTES = 67_043_328


def fast_shards(n, alignment, pair_rep, align_gain, align_offset, left_weight, right_weight, *layer_params):
    seq, residues, channels = alignment.shape
    lay = Layout(n, seq, residues, pair_rep.shape[0], left_weight.shape[1])
    f32, bf16 = jnp.float32, jnp.bfloat16
    me = lax.axis_index("row")
    place = jnp.stack([me // CORES, me % CORES]).astype(jnp.int32)
    sent = pl.pallas_call(
        functools.partial(send_kernel, lay),
        out_shape=[jax.ShapeDtypeStruct((lay.total(k), LANES), bf16) for k in range(lay.chips)],
        in_specs=[SMEM] + [VMEM] * 6,
        out_specs=[VMEM] * lay.chips,
        scratch_shapes=[
            pltpu.VMEM((channels // LANES, seq * residues, LANES), f32),
            pltpu.VMEM((seq * lay.proj, LANES), f32),
        ],
        compiler_params=pltpu.CompilerParams(vmem_limit_bytes=VMEM_BYTES - sum(map(lay.total, range(lay.chips))) * 2 * LANES - 150_000),
        name="send",
    )(
        place,
        alignment,
        pair_rep,
        align_gain.reshape(1, -1),
        align_offset.reshape(1, -1),
        left_weight.T,
        right_weight.T,
    )

    def permute(x, k):
        return lax.ppermute(x, "row", [(d, d ^ k) for d in range(n)])

    got = {k: permute(sent[k], CORES * k) if k else sent[0] for k in range(lay.chips)}
    relayed = {k: permute(got[k ^ 1][: lay.relayed], CORES) for k in range(lay.chips) if lay.pair_only(k)}
    operands, outers, pairs = [], [], []

    def take(x, k, core, outer, pair):
        if outer is not None:
            outers.append((len(operands), outer))
        if pair is not None:
            pairs.append((len(operands), pair, CORES * k + core))
        operands.append(x)

    for k in range(lay.chips):
        outer = None if lay.pair_only(k) else lay.right_at(k)
        take(got[k], k, 0, outer, lay.pair_at(k))
        take(permute(got[k], 1), k, 1, outer, lay.pair_at(k))
        if k in relayed:
            take(relayed[k], k, 0, lay.left, None)
            take(permute(relayed[k], 1), k, 1, lay.left, None)
    ow, ob, pg, ps, uw, ub, dw, db = layer_params
    rows_j = lay.rows
    return pl.pallas_call(
        functools.partial(update_kernel, lay, outers, pairs),
        out_shape=jax.ShapeDtypeStruct((rows_j, residues, LANES), bf16),
        in_specs=[SMEM] + [VMEM] * (len(operands) + 8),
        out_specs=VMEM,
        scratch_shapes=[
            pltpu.VMEM((lay.proj * lay.proj, rows_j * residues), bf16),
            pltpu.VMEM((rows_j, residues, LANES), f32),
        ],
        compiler_params=pltpu.CompilerParams(vmem_limit_bytes=16 * MIB),
        name="update",
    )(
        place,
        *operands,
        ow,
        ob.reshape(1, -1),
        pg.reshape(1, -1),
        ps.reshape(1, -1),
        uw,
        ub.reshape(1, -1),
        dw,
        db.reshape(1, -1),
    )


def fits(n, alignment, pair_rep, left_weight):
    seq, residues, _ = alignment.shape
    rows, _, width = pair_rep.shape
    return (
        n >= 8
        and n & (n - 1) == 0
        and seq == 8
        and rows == 8
        and residues == LANES
        and width == LANES
        and left_weight.shape[1] == 32
    )


def solution(mesh):
    n = mesh.shape["row"]

    def shards(alignment, pair_rep, align_gain, align_offset, left_weight, right_weight, *layer_params):
        if fits(n, alignment, pair_rep, left_weight):
            return fast_shards(n, alignment, pair_rep, align_gain, align_offset, left_weight, right_weight, *layer_params)
        return plain_shards(alignment, pair_rep, align_gain, align_offset, left_weight, right_weight, *layer_params)

    split = P(("group", "row"), None, None)
    return jax.shard_map(
        shards,
        mesh=mesh,
        in_specs=(split, split) + (P(),) * 12,
        out_specs=split,
        check_vma=False,
    )
```

```python
import functools

import jax
import jax.numpy as jnp
from jax import lax
from jax.experimental import pallas as pl
from jax.experimental.pallas import tpu as pltpu
from jax.sharding import PartitionSpec as P


epsilon = 1e-05
LANES = 128
CORES = 2


VMEM = pl.BlockSpec(memory_space=pltpu.VMEM)
SMEM = pl.BlockSpec(memory_space=pltpu.SMEM)
HBM = pl.BlockSpec(memory_space=pltpu.HBM)


def layer_norm(values, gain, shift):
    values = values.astype(jnp.float32)
    center = jnp.mean(values, axis=-1, keepdims=True)
    spread = jnp.mean(jnp.square(values - center), axis=-1, keepdims=True)
    return (values - center) * lax.rsqrt(spread + epsilon) * gain + shift


def pair_update(left_flat, right_flat, pair_tile, layer_params, proj_w):
    outer_weight, outer_bias, pair_gain, pair_shift, up_weight, up_bias, down_weight, down_bias = (
        layer_params
    )
    rows_i = left_flat.shape[0]
    rows_j = right_flat.shape[0]
    width = outer_weight.shape[1]
    seq_total = left_flat.shape[1] // proj_w
    left_rows = left_flat.reshape(rows_i, seq_total, proj_w)
    right_rows = right_flat.reshape(rows_j, seq_total, proj_w)
    outer_mean = jnp.einsum(
        "isc,jse->ijce", left_rows, right_rows, preferred_element_type=jnp.float32
    ) * (1.0 / seq_total)
    outer_mean = outer_mean.astype(jnp.bfloat16).reshape(rows_i * rows_j, proj_w * proj_w)
    summed = (
        pair_tile.reshape(rows_i * rows_j, width).astype(jnp.float32)
        + jnp.dot(outer_mean, outer_weight, preferred_element_type=jnp.float32)
        + outer_bias
    )
    normed = layer_norm(summed, pair_gain, pair_shift).astype(jnp.bfloat16)
    hidden = jax.nn.relu(
        jnp.dot(normed, up_weight, preferred_element_type=jnp.float32) + up_bias
    ).astype(jnp.bfloat16)
    result = summed + jnp.dot(hidden, down_weight, preferred_element_type=jnp.float32) + down_bias
    return result.astype(jnp.bfloat16).reshape(rows_i, rows_j, width)


def in_blocks(amount, builder):
    if amount > 256 and amount % 256 == 0:
        stacked = lax.map(
            lambda which_k: builder(which_k * 256, 256), jnp.arange(amount // 256, dtype=jnp.int32)
        )
        return stacked.reshape((amount,) + stacked.shape[2:])
    return builder(0, amount)


def plain_shards(alignment, pair_rep, align_gain, align_offset, left_weight, right_weight, *layer_params):
    proj_w = left_weight.shape[1]
    normed = layer_norm(alignment, align_gain, align_offset).astype(jnp.bfloat16)
    both = [
        jnp.einsum("src,cd->rsd", normed, weight, preferred_element_type=jnp.float32).astype(jnp.bfloat16)
        for weight in (left_weight, right_weight)
    ]
    left, right = [
        lax.all_to_all(x, "row", split_axis=0, concat_axis=1, tiled=True).reshape(
            x.shape[0] // lax.axis_size("row"), -1
        )
        for x in both
    ]
    pieces = lax.all_gather(right, "row", axis=0, tiled=True)

    def builder(start, amount):
        segment = lax.dynamic_slice_in_dim(pieces, start, amount, 0)
        pair_tile = lax.dynamic_slice_in_dim(pair_rep, start, amount, 1)
        return jnp.transpose(pair_update(left, segment, pair_tile, layer_params, proj_w), (1, 0, 2))

    columns = in_blocks(pieces.shape[0], builder)
    return lax.all_to_all(columns, "row", split_axis=0, concat_axis=1, tiled=True)


class Layout:
    def __init__(self, n, seq, residues, own_rows, proj_w):
        self.n, self.chips = n, n // CORES
        self.far = self.chips // 2
        self.seq, self.residues, self.rows, self.proj = seq, residues, own_rows, proj_w
        self.per = 16 // seq
        self.fold = LANES // proj_w
        self.chip_rows = CORES * own_rows
        self.left = proj_w * seq
        self.right = self.chip_rows // self.fold * seq
        self.pair = self.chip_rows * own_rows
        self.relayed = self.left + self.right

    def crosses(self, k):
        return k >= self.far and k % 2 == 0

    def right_at(self, k):
        return self.left + (self.right if self.crosses(k) else 0)

    def pair_at(self, k):
        return 0 if self.pair_only(k) else self.right_at(k) + self.right

    def pair_only(self, k):
        return k >= self.far and k % 2 == 1

    def total(self, k):
        return self.pair_at(k) + self.pair


def send_kernel(lay, place, x_ref, pair_ref, gain_ref, offset_ref, wl_ref, wr_ref, *rest):
    bufs, (norm_ref, left_ref) = rest[: lay.chips], rest[lay.chips :]
    seq, residues, proj, fold = lay.seq, lay.residues, lay.proj, lay.fold
    f32, bf16 = jnp.float32, jnp.bfloat16
    halves = norm_ref.shape[0]
    nt = (((1,), (1,)), ((), ()))
    x = x_ref[...].reshape(seq * residues, x_ref.shape[2])
    normed = layer_norm(x, gain_ref[...], offset_ref[...])
    for h in range(halves):
        norm_ref[h] = normed[:, h * LANES : (h + 1) * LANES]
    left = lax.dot_general(wl_ref[...], normed.astype(bf16), nt, preferred_element_type=f32)
    for s in range(seq):
        left_ref[s * proj : (s + 1) * proj, :] = left[:, s * residues : (s + 1) * residues]
    for tile in range(proj // lay.per):
        rows = jnp.concatenate(
            [left_ref[pl.ds(tile * lay.per + b, seq, stride=proj), :] for b in range(lay.per)], axis=0
        ).astype(bf16)
        for k, buf in enumerate(bufs):
            if not lay.pair_only(k):
                buf[tile * 16 : (tile + 1) * 16, :] = rows
    groups = residues // fold
    wr = wr_ref[...]
    zero = jnp.zeros_like(wr)
    right = None
    for g in range(fold):
        rows = jnp.concatenate(
            [
                jnp.concatenate(
                    [norm_ref[h, pl.ds(u * fold + g, seq, stride=residues), :] for u in range(groups)], axis=0
                )
                for h in range(halves)
            ],
            axis=1,
        ).astype(bf16)
        weight = jnp.concatenate([wr if h == g else zero for h in range(fold)], axis=0)
        part = lax.dot_general(rows, weight, nt, preferred_element_type=f32)
        right = part if right is None else right + part
    left_ref[...] = right

    def right_of(k):
        at = pl.multiple_of(lax.bitwise_xor(place[0], k) * lay.right, lay.right)
        return left_ref[pl.ds(at, lay.right), :].astype(bf16)

    for k, buf in enumerate(bufs):
        if not lay.pair_only(k):
            at = lay.right_at(k)
            buf[at : at + lay.right, :] = right_of(k)
        if lay.crosses(k):
            buf[lay.left : lay.left + lay.right, :] = right_of(k ^ 1)
        at = pl.multiple_of(lax.bitwise_xor(place[0], k) * lay.chip_rows, lay.chip_rows)
        tile = pair_ref[:, pl.ds(at, lay.chip_rows), :].astype(f32)
        tile = jnp.swapaxes(tile, 0, 1).reshape(lay.pair, LANES)
        at = lay.pair_at(k)
        buf[at : at + lay.pair, :] = tile.astype(bf16)


def update_kernel(lay, outers, pairs, place, *rest):
    count = max([b for b, _ in outers] + [b for b, _, _ in pairs]) + 1
    bufs = rest[:count]
    (ow_ref, ob_ref, pg_ref, ps_ref, uw_ref, ub_ref, dw_ref, db_ref, out_ref, outer_ref, pair_ref) = rest[count:]
    seq, residues, proj, rows_j, fold, per = lay.seq, lay.residues, lay.proj, lay.rows, lay.fold, lay.per
    f32, bf16 = jnp.float32, jnp.bfloat16
    chip, core = place[0], place[1]
    groups = rows_j // fold
    own = pl.multiple_of(core * (groups * seq), groups * seq)
    spread = []
    for b in range(per):
        rows = []
        for m, at in outers:
            got = bufs[m][pl.ds(at + own, groups * seq), :].astype(f32)
            got = jnp.concatenate([got[u * seq : (u + 1) * seq] for u in range(groups)], axis=1)
            zero = jnp.zeros_like(got)
            rows += [got if h == b else zero for h in range(per)]
        spread.append(jnp.concatenate(rows, axis=0).T.astype(bf16))
    right = jnp.concatenate(spread, axis=0)
    wide = 2
    scale = 1.0 / (seq * lay.n)
    for tile in range(0, proj // per, wide):
        left = jnp.concatenate(
            [
                jnp.concatenate([bufs[m][t * 16 : (t + 1) * 16, :] for m, _ in outers], axis=0)
                for t in range(tile, tile + wide)
            ],
            axis=1,
        )
        x = (jnp.dot(right, left, preferred_element_type=f32) * scale).astype(bf16)
        for b in range(per):
            for w in range(wide):
                c = (tile + w) * per + b
                for j in range(rows_j):
                    at = (b * rows_j + j) * proj
                    outer_ref[c * proj : (c + 1) * proj, j * residues : (j + 1) * residues] = x[
                        at : at + proj, w * residues : (w + 1) * residues
                    ]
    own = pl.multiple_of(core * (rows_j * rows_j), rows_j * rows_j)
    for m, at, k in pairs:
        sender = lax.bitwise_xor(chip * CORES + core, k)
        got = bufs[m][pl.ds(at + own, rows_j * rows_j), :].astype(f32)
        for j in range(rows_j):
            pair_ref[j, pl.ds(pl.multiple_of(sender * rows_j, rows_j), rows_j), :] = got[j * rows_j : (j + 1) * rows_j]
    added = lax.dot_general(ow_ref[...], outer_ref[...], (((0,), (0,)), ((), ())), preferred_element_type=f32)
    step = 4
    for j0 in range(0, rows_j, step):
        summed = jnp.concatenate(
            [added[:, j * residues : (j + 1) * residues].T + pair_ref[j] for j in range(j0, j0 + step)], axis=0
        )
        summed = summed + ob_ref[...]
        normed = layer_norm(summed, pg_ref[...], ps_ref[...]).astype(bf16)
        hidden = jnp.dot(normed, uw_ref[...], preferred_element_type=f32) + ub_ref[...]
        hidden = jnp.maximum(hidden, 0.0).astype(bf16)
        result = summed + jnp.dot(hidden, dw_ref[...], preferred_element_type=f32) + db_ref[...]
        out_ref[j0 : j0 + step] = result.astype(bf16).reshape(step, residues, LANES)


MIB = 1 << 20


def in_hbm(x):
    return pltpu.with_memory_space_constraint(x, pltpu.HBM)


def in_vmem(x):
    return pltpu.with_memory_space_constraint(x, pltpu.VMEM)


def load_kernel(*refs):
    count = len(refs) // 2
    for source, to in zip(refs[:count], refs[count:]):
        to[...] = source[...]


def load(arrays):
    return pl.pallas_call(
        load_kernel,
        out_shape=[jax.ShapeDtypeStruct(a.shape, a.dtype) for a in arrays],
        in_specs=[VMEM] * len(arrays),
        out_specs=[VMEM] * len(arrays),
        compiler_params=pltpu.CompilerParams(vmem_limit_bytes=4 * MIB),
        name="load",
    )(*[in_hbm(a) for a in arrays])


def fast_shards(n, alignment, pair_rep, align_gain, align_offset, left_weight, right_weight, *layer_params):
    seq, residues, channels = alignment.shape
    lay = Layout(n, seq, residues, pair_rep.shape[0], left_weight.shape[1])
    f32, bf16 = jnp.float32, jnp.bfloat16
    me = lax.axis_index("row")
    place = jnp.stack([me // CORES, me % CORES]).astype(jnp.int32)
    sent = pl.pallas_call(
        functools.partial(send_kernel, lay),
        out_shape=[jax.ShapeDtypeStruct((lay.total(k), LANES), bf16) for k in range(lay.chips)],
        in_specs=[SMEM] + [VMEM] * 6,
        out_specs=[VMEM] * lay.chips,
        scratch_shapes=[
            pltpu.VMEM((channels // LANES, seq * residues, LANES), f32),
            pltpu.VMEM((seq * lay.proj, LANES), f32),
        ],
        compiler_params=pltpu.CompilerParams(vmem_limit_bytes=8 * MIB),
        name="send",
    )(
        place,
        in_hbm(alignment),
        in_hbm(pair_rep),
        in_hbm(align_gain.reshape(1, -1)),
        in_hbm(align_offset.reshape(1, -1)),
        in_hbm(left_weight.T),
        in_hbm(right_weight.T),
    )

    def permute(x, k):
        return lax.ppermute(x, "row", [(d, d ^ k) for d in range(n)])

    got = {k: permute(sent[k], CORES * k) if k else sent[0] for k in range(lay.chips)}
    relayed = {k: permute(got[k ^ 1][: lay.relayed], CORES) for k in range(lay.chips) if lay.pair_only(k)}
    operands, outers, pairs = [], [], []

    def take(x, k, core, outer, pair):
        if outer is not None:
            outers.append((len(operands), outer))
        if pair is not None:
            pairs.append((len(operands), pair, CORES * k + core))
        operands.append(x)

    for k in range(lay.chips):
        outer = None if lay.pair_only(k) else lay.right_at(k)
        take(got[k], k, 0, outer, lay.pair_at(k))
        take(permute(got[k], 1), k, 1, outer, lay.pair_at(k))
        if k in relayed:
            take(relayed[k], k, 0, lay.left, None)
            take(permute(relayed[k], 1), k, 1, lay.left, None)
    params = load([p if p.ndim == 2 else p.reshape(1, -1) for p in layer_params])
    rows_j = lay.rows
    return pl.pallas_call(
        functools.partial(update_kernel, lay, outers, pairs),
        out_shape=jax.ShapeDtypeStruct((rows_j, residues, LANES), bf16),
        in_specs=[SMEM] + [VMEM] * (len(operands) + 8),
        out_specs=VMEM,
        scratch_shapes=[
            pltpu.VMEM((lay.proj * lay.proj, rows_j * residues), bf16),
            pltpu.VMEM((rows_j, residues, LANES), f32),
        ],
        compiler_params=pltpu.CompilerParams(vmem_limit_bytes=16 * MIB),
        name="update",
    )(
        place,
        *[in_vmem(x) for x in operands],
        *[in_vmem(x) for x in params],
    )


def fits(n, alignment, pair_rep, left_weight):
    seq, residues, _ = alignment.shape
    rows, _, width = pair_rep.shape
    return (
        n >= 8
        and n & (n - 1) == 0
        and seq == 8
        and rows == 8
        and residues == LANES
        and width == LANES
        and left_weight.shape[1] == 32
    )


def solution(mesh):
    n = mesh.shape["row"]

    def shards(alignment, pair_rep, align_gain, align_offset, left_weight, right_weight, *layer_params):
        if fits(n, alignment, pair_rep, left_weight):
            return fast_shards(n, alignment, pair_rep, align_gain, align_offset, left_weight, right_weight, *layer_params)
        return plain_shards(alignment, pair_rep, align_gain, align_offset, left_weight, right_weight, *layer_params)

    split = P(("group", "row"), None, None)
    return jax.shard_map(
        shards,
        mesh=mesh,
        in_specs=(split, split) + (P(),) * 12,
        out_specs=split,
        check_vma=False,
    )
```

```python
import functools

import jax
import jax.numpy as jnp
from jax import lax
from jax.experimental import pallas as pl
from jax.experimental.pallas import tpu as pltpu
from jax.sharding import PartitionSpec as P


epsilon = 1e-05
LANES = 128
CORES = 2


VMEM = pl.BlockSpec(memory_space=pltpu.VMEM)
SMEM = pl.BlockSpec(memory_space=pltpu.SMEM)
HBM = pl.BlockSpec(memory_space=pltpu.HBM)


def layer_norm(values, gain, shift):
    values = values.astype(jnp.float32)
    center = jnp.mean(values, axis=-1, keepdims=True)
    spread = jnp.mean(jnp.square(values - center), axis=-1, keepdims=True)
    return (values - center) * lax.rsqrt(spread + epsilon) * gain + shift


def pair_update(left_flat, right_flat, pair_tile, layer_params, proj_w):
    outer_weight, outer_bias, pair_gain, pair_shift, up_weight, up_bias, down_weight, down_bias = (
        layer_params
    )
    rows_i = left_flat.shape[0]
    rows_j = right_flat.shape[0]
    width = outer_weight.shape[1]
    seq_total = left_flat.shape[1] // proj_w
    left_rows = left_flat.reshape(rows_i, seq_total, proj_w)
    right_rows = right_flat.reshape(rows_j, seq_total, proj_w)
    outer_mean = jnp.einsum(
        "isc,jse->ijce", left_rows, right_rows, preferred_element_type=jnp.float32
    ) * (1.0 / seq_total)
    outer_mean = outer_mean.astype(jnp.bfloat16).reshape(rows_i * rows_j, proj_w * proj_w)
    summed = (
        pair_tile.reshape(rows_i * rows_j, width).astype(jnp.float32)
        + jnp.dot(outer_mean, outer_weight, preferred_element_type=jnp.float32)
        + outer_bias
    )
    normed = layer_norm(summed, pair_gain, pair_shift).astype(jnp.bfloat16)
    hidden = jax.nn.relu(
        jnp.dot(normed, up_weight, preferred_element_type=jnp.float32) + up_bias
    ).astype(jnp.bfloat16)
    result = summed + jnp.dot(hidden, down_weight, preferred_element_type=jnp.float32) + down_bias
    return result.astype(jnp.bfloat16).reshape(rows_i, rows_j, width)


def in_blocks(amount, builder):
    if amount > 256 and amount % 256 == 0:
        stacked = lax.map(
            lambda which_k: builder(which_k * 256, 256), jnp.arange(amount // 256, dtype=jnp.int32)
        )
        return stacked.reshape((amount,) + stacked.shape[2:])
    return builder(0, amount)


def plain_shards(alignment, pair_rep, align_gain, align_offset, left_weight, right_weight, *layer_params):
    proj_w = left_weight.shape[1]
    normed = layer_norm(alignment, align_gain, align_offset).astype(jnp.bfloat16)
    both = [
        jnp.einsum("src,cd->rsd", normed, weight, preferred_element_type=jnp.float32).astype(jnp.bfloat16)
        for weight in (left_weight, right_weight)
    ]
    left, right = [
        lax.all_to_all(x, "row", split_axis=0, concat_axis=1, tiled=True).reshape(
            x.shape[0] // lax.axis_size("row"), -1
        )
        for x in both
    ]
    pieces = lax.all_gather(right, "row", axis=0, tiled=True)

    def builder(start, amount):
        segment = lax.dynamic_slice_in_dim(pieces, start, amount, 0)
        pair_tile = lax.dynamic_slice_in_dim(pair_rep, start, amount, 1)
        return jnp.transpose(pair_update(left, segment, pair_tile, layer_params, proj_w), (1, 0, 2))

    columns = in_blocks(pieces.shape[0], builder)
    return lax.all_to_all(columns, "row", split_axis=0, concat_axis=1, tiled=True)


class Layout:
    def __init__(self, n, seq, residues, own_rows, proj_w):
        self.n, self.chips = n, n // CORES
        self.far = self.chips // 2
        self.seq, self.residues, self.rows, self.proj = seq, residues, own_rows, proj_w
        self.per = 16 // seq
        self.fold = LANES // proj_w
        self.chip_rows = CORES * own_rows
        self.left = proj_w * seq
        self.right = self.chip_rows // self.fold * seq
        self.pair = self.chip_rows * own_rows
        self.targets = list(range(self.chips))

    def sent(self, k):
        return ([("left", k)] if k <= self.far else []) + [("right", k), ("pair", k)]

    def rows_of(self, parts):
        return sum(getattr(self, what) for what, _ in parts)

    def at(self, k, what, to):
        parts = self.sent(k)
        return self.rows_of(parts[: parts.index((what, to))])

    def total(self, k):
        return self.rows_of(self.sent(k))


def send_kernel(lay, place, x_ref, pair_ref, gain_ref, offset_ref, wl_ref, wr_ref, *rest):
    bufs, (left_ref, right_ref) = dict(zip(lay.targets, rest)), rest[len(lay.targets) :]
    seq, residues, proj, fold = lay.seq, lay.residues, lay.proj, lay.fold
    f32, bf16 = jnp.float32, jnp.bfloat16
    nt = (((1,), (1,)), ((), ()))
    x = x_ref[...].reshape(seq * residues, x_ref.shape[2])
    normed = layer_norm(x, gain_ref[...], offset_ref[...]).astype(bf16)
    left = lax.dot_general(wl_ref[...], normed, nt, preferred_element_type=f32)
    for s in range(seq):
        left_ref[s * proj : (s + 1) * proj, :] = left[:, s * residues : (s + 1) * residues]
    for tile in range(proj // lay.per):
        rows = jnp.concatenate(
            [left_ref[pl.ds(tile * lay.per + b, seq, stride=proj), :] for b in range(lay.per)], axis=0
        ).astype(bf16)
        for k, buf in bufs.items():
            if ("left", k) in lay.sent(k):
                buf[tile * 16 : (tile + 1) * 16, :] = rows
    groups = residues // fold
    wide = jnp.concatenate([wr_ref[...]] * fold, axis=0)
    right = lax.dot_general(normed, wide, nt, preferred_element_type=f32)
    row = lax.broadcasted_iota(jnp.int32, (residues, LANES), 0)
    lane = lax.broadcasted_iota(jnp.int32, (residues, LANES), 1)
    keep = lax.rem(row, fold) == lax.div(lane, proj)
    row = lax.broadcasted_iota(jnp.int32, (groups, residues), 0)
    lane = lax.broadcasted_iota(jnp.int32, (groups, residues), 1)
    stack = jnp.where(lax.div(lane, fold) == row, 1.0, 0.0).astype(bf16)
    for s in range(seq):
        own = jnp.where(keep, right[s * residues : (s + 1) * residues], 0.0).astype(bf16)
        right_ref[s * groups : (s + 1) * groups, :] = jnp.dot(stack, own, preferred_element_type=f32)

    def right_of(k):
        at = lax.bitwise_xor(place[0], k) * (lay.right // seq)
        rows = [right_ref[pl.ds(at + u, seq, stride=groups), :] for u in range(lay.right // seq)]
        return jnp.concatenate(rows, axis=0).astype(bf16)

    def pair_of(k):
        at = pl.multiple_of(lax.bitwise_xor(place[0], k) * lay.chip_rows, lay.chip_rows)
        tile = pair_ref[:, pl.ds(at, lay.chip_rows), :].astype(f32)
        return jnp.swapaxes(tile, 0, 1).reshape(lay.pair, LANES).astype(bf16)

    for k, buf in bufs.items():
        for what, to in lay.sent(k):
            at = lay.at(k, what, to)
            if what == "right":
                buf[at : at + lay.right, :] = right_of(to)
            if what == "pair":
                buf[at : at + lay.pair, :] = pair_of(to)


def update_kernel(lay, outers, pairs, place, *rest):
    count = max([m for own in outers for m, _ in own] + [m for m, _, _ in pairs]) + 1
    bufs = rest[:count]
    (ow_ref, ob_ref, pg_ref, ps_ref, uw_ref, ub_ref, dw_ref, db_ref, out_ref, outer_ref, pair_ref) = rest[count:]
    seq, residues, proj, rows_j, fold, per = lay.seq, lay.residues, lay.proj, lay.rows, lay.fold, lay.per
    f32, bf16 = jnp.float32, jnp.bfloat16
    chip, core = place[0], place[1]
    groups = rows_j // fold
    own = pl.multiple_of(core * (groups * seq), groups * seq)
    spread = []
    for b in range(per):
        rows = []
        for _, (m, at) in outers:
            got = bufs[m][pl.ds(at + own, groups * seq), :].astype(f32)
            got = jnp.concatenate([got[u * seq : (u + 1) * seq] for u in range(groups)], axis=1)
            zero = jnp.zeros_like(got)
            rows += [got if h == b else zero for h in range(per)]
        spread.append(jnp.concatenate(rows, axis=0).T.astype(bf16))
    right = jnp.concatenate(spread, axis=0)
    wide = 2
    scale = 1.0 / (seq * lay.n)
    for tile in range(0, proj // per, wide):
        left = jnp.concatenate(
            [
                jnp.concatenate([bufs[m][at + t * 16 : at + (t + 1) * 16, :] for (m, at), _ in outers], axis=0)
                for t in range(tile, tile + wide)
            ],
            axis=1,
        )
        x = (jnp.dot(right, left, preferred_element_type=f32) * scale).astype(bf16)
        for b in range(per):
            for w in range(wide):
                c = (tile + w) * per + b
                for j in range(rows_j):
                    at = (b * rows_j + j) * proj
                    outer_ref[c * proj : (c + 1) * proj, j * residues : (j + 1) * residues] = x[
                        at : at + proj, w * residues : (w + 1) * residues
                    ]
    own = pl.multiple_of(core * (rows_j * rows_j), rows_j * rows_j)
    for m, at, k in pairs:
        sender = lax.bitwise_xor(chip * CORES + core, k)
        got = bufs[m][pl.ds(at + own, rows_j * rows_j), :].astype(f32)
        for j in range(rows_j):
            pair_ref[j, pl.ds(pl.multiple_of(sender * rows_j, rows_j), rows_j), :] = got[j * rows_j : (j + 1) * rows_j]
    added = lax.dot_general(ow_ref[...], outer_ref[...], (((0,), (0,)), ((), ())), preferred_element_type=f32)
    step = 4
    for j0 in range(0, rows_j, step):
        summed = jnp.concatenate(
            [added[:, j * residues : (j + 1) * residues].T + pair_ref[j] for j in range(j0, j0 + step)], axis=0
        )
        summed = summed + ob_ref[...]
        normed = layer_norm(summed, pg_ref[...], ps_ref[...]).astype(bf16)
        hidden = jnp.dot(normed, uw_ref[...], preferred_element_type=f32) + ub_ref[...]
        hidden = jnp.maximum(hidden, 0.0).astype(bf16)
        result = summed + jnp.dot(hidden, dw_ref[...], preferred_element_type=f32) + db_ref[...]
        out_ref[j0 : j0 + step] = result.astype(bf16).reshape(step, residues, LANES)


MIB = 1 << 20


def in_hbm(x):
    return pltpu.with_memory_space_constraint(x, pltpu.HBM)


def in_vmem(x):
    return pltpu.with_memory_space_constraint(x, pltpu.VMEM)


def load_kernel(*refs):
    count = len(refs) // 2
    for source, to in zip(refs[:count], refs[count:]):
        to[...] = source[...]


def load(arrays):
    return pl.pallas_call(
        load_kernel,
        out_shape=[jax.ShapeDtypeStruct(a.shape, a.dtype) for a in arrays],
        in_specs=[VMEM] * len(arrays),
        out_specs=[VMEM] * len(arrays),
        compiler_params=pltpu.CompilerParams(vmem_limit_bytes=4 * MIB),
        name="load",
    )(*[in_hbm(a) for a in arrays])


def fast_shards(n, alignment, pair_rep, align_gain, align_offset, left_weight, right_weight, *layer_params):
    seq, residues, _ = alignment.shape
    lay = Layout(n, seq, residues, pair_rep.shape[0], left_weight.shape[1])
    f32, bf16 = jnp.float32, jnp.bfloat16
    me = lax.axis_index("row")
    place = jnp.stack([me // CORES, me % CORES]).astype(jnp.int32)
    sent = pl.pallas_call(
        functools.partial(send_kernel, lay),
        out_shape=[jax.ShapeDtypeStruct((lay.total(k), LANES), bf16) for k in lay.targets],
        in_specs=[SMEM] + [VMEM] * 6,
        out_specs=[VMEM] * len(lay.targets),
        scratch_shapes=[
            pltpu.VMEM((seq * lay.proj, LANES), f32),
            pltpu.VMEM((seq * (residues // lay.fold), LANES), f32),
        ],
        compiler_params=pltpu.CompilerParams(vmem_limit_bytes=8 * MIB),
        name="send",
    )(
        place,
        in_hbm(alignment),
        in_hbm(pair_rep),
        in_hbm(align_gain.reshape(1, -1)),
        in_hbm(align_offset.reshape(1, -1)),
        in_hbm(left_weight.T),
        in_hbm(right_weight.T),
    )

    def permute(x, k):
        return lax.ppermute(x, "row", [(d, d ^ k) for d in range(n)])

    arrays = {f"go{k}": permute(x, CORES * k) if k else x for k, x in zip(lay.targets, sent)}
    find = {}
    for k in lay.targets:
        for what, to in lay.sent(k):
            if to == k:
                find[what, k] = (f"go{k}", lay.at(k, what, k))
    far = lay.far
    lefts = {far: arrays[f"go{far}"][: lay.left]}
    for k in range(far + 2, lay.chips, 2):
        lefts[k] = permute(lefts[far], CORES * (k ^ far))
    for k in range(far + 1, lay.chips, 2):
        lefts[k] = permute(lefts[k ^ 1], CORES)
    for k in range(far + 1, lay.chips):
        arrays[f"left{k}"] = lefts[k]
        find["left", k] = (f"left{k}", 0)
    operands, spot = [], {}
    for name, x in arrays.items():
        for core in range(CORES):
            spot[name, core] = len(operands)
            operands.append(permute(x, 1) if core else x)

    def where(what, k, core):
        name, at = find[what, k]
        return spot[name, core], at

    senders = [(k, core) for core in range(CORES) for k in range(lay.chips)]
    outers = [(where("left", *m), where("right", *m)) for m in senders]
    pairs = [where("pair", *m) + (CORES * m[0] + m[1],) for m in senders]
    params = load([p if p.ndim == 2 else p.reshape(1, -1) for p in layer_params])
    rows_j = lay.rows
    return pl.pallas_call(
        functools.partial(update_kernel, lay, outers, pairs),
        out_shape=jax.ShapeDtypeStruct((rows_j, residues, LANES), bf16),
        in_specs=[SMEM] + [VMEM] * (len(operands) + 8),
        out_specs=VMEM,
        scratch_shapes=[
            pltpu.VMEM((lay.proj * lay.proj, rows_j * residues), bf16),
            pltpu.VMEM((rows_j, residues, LANES), f32),
        ],
        compiler_params=pltpu.CompilerParams(vmem_limit_bytes=16 * MIB),
        name="update",
    )(
        place,
        *[in_vmem(x) for x in operands],
        *[in_vmem(x) for x in params],
    )


def fits(n, alignment, pair_rep, left_weight):
    seq, residues, _ = alignment.shape
    rows, _, width = pair_rep.shape
    return (
        n >= 8
        and n & (n - 1) == 0
        and seq == 8
        and rows == 8
        and residues == LANES
        and width == LANES
        and left_weight.shape[1] == 32
    )


def solution(mesh):
    n = mesh.shape["row"]

    def shards(alignment, pair_rep, align_gain, align_offset, left_weight, right_weight, *layer_params):
        if fits(n, alignment, pair_rep, left_weight):
            return fast_shards(n, alignment, pair_rep, align_gain, align_offset, left_weight, right_weight, *layer_params)
        return plain_shards(alignment, pair_rep, align_gain, align_offset, left_weight, right_weight, *layer_params)

    split = P(("group", "row"), None, None)
    return jax.shard_map(
        shards,
        mesh=mesh,
        in_specs=(split, split) + (P(),) * 12,
        out_specs=split,
        check_vma=False,
    )
```

```python
import functools

import jax
import jax.numpy as jnp
from jax import lax
from jax.experimental import pallas as pl
from jax.experimental.pallas import tpu as pltpu
from jax.sharding import PartitionSpec as P


epsilon = 1e-05
LANES = 128
CORES = 2


VMEM = pl.BlockSpec(memory_space=pltpu.VMEM)
SMEM = pl.BlockSpec(memory_space=pltpu.SMEM)
HBM = pl.BlockSpec(memory_space=pltpu.HBM)


def layer_norm(values, gain, shift):
    values = values.astype(jnp.float32)
    center = jnp.mean(values, axis=-1, keepdims=True)
    spread = jnp.mean(jnp.square(values - center), axis=-1, keepdims=True)
    return (values - center) * lax.rsqrt(spread + epsilon) * gain + shift


def pair_update(left_flat, right_flat, pair_tile, layer_params, proj_w):
    outer_weight, outer_bias, pair_gain, pair_shift, up_weight, up_bias, down_weight, down_bias = (
        layer_params
    )
    rows_i = left_flat.shape[0]
    rows_j = right_flat.shape[0]
    width = outer_weight.shape[1]
    seq_total = left_flat.shape[1] // proj_w
    left_rows = left_flat.reshape(rows_i, seq_total, proj_w)
    right_rows = right_flat.reshape(rows_j, seq_total, proj_w)
    outer_mean = jnp.einsum(
        "isc,jse->ijce", left_rows, right_rows, preferred_element_type=jnp.float32
    ) * (1.0 / seq_total)
    outer_mean = outer_mean.astype(jnp.bfloat16).reshape(rows_i * rows_j, proj_w * proj_w)
    summed = (
        pair_tile.reshape(rows_i * rows_j, width).astype(jnp.float32)
        + jnp.dot(outer_mean, outer_weight, preferred_element_type=jnp.float32)
        + outer_bias
    )
    normed = layer_norm(summed, pair_gain, pair_shift).astype(jnp.bfloat16)
    hidden = jax.nn.relu(
        jnp.dot(normed, up_weight, preferred_element_type=jnp.float32) + up_bias
    ).astype(jnp.bfloat16)
    result = summed + jnp.dot(hidden, down_weight, preferred_element_type=jnp.float32) + down_bias
    return result.astype(jnp.bfloat16).reshape(rows_i, rows_j, width)


def in_blocks(amount, builder):
    if amount > 256 and amount % 256 == 0:
        stacked = lax.map(
            lambda which_k: builder(which_k * 256, 256), jnp.arange(amount // 256, dtype=jnp.int32)
        )
        return stacked.reshape((amount,) + stacked.shape[2:])
    return builder(0, amount)


def plain_shards(alignment, pair_rep, align_gain, align_offset, left_weight, right_weight, *layer_params):
    proj_w = left_weight.shape[1]
    normed = layer_norm(alignment, align_gain, align_offset).astype(jnp.bfloat16)
    both = [
        jnp.einsum("src,cd->rsd", normed, weight, preferred_element_type=jnp.float32).astype(jnp.bfloat16)
        for weight in (left_weight, right_weight)
    ]
    left, right = [
        lax.all_to_all(x, "row", split_axis=0, concat_axis=1, tiled=True).reshape(
            x.shape[0] // lax.axis_size("row"), -1
        )
        for x in both
    ]
    pieces = lax.all_gather(right, "row", axis=0, tiled=True)

    def builder(start, amount):
        segment = lax.dynamic_slice_in_dim(pieces, start, amount, 0)
        pair_tile = lax.dynamic_slice_in_dim(pair_rep, start, amount, 1)
        return jnp.transpose(pair_update(left, segment, pair_tile, layer_params, proj_w), (1, 0, 2))

    columns = in_blocks(pieces.shape[0], builder)
    return lax.all_to_all(columns, "row", split_axis=0, concat_axis=1, tiled=True)


class Layout:
    def __init__(self, n, seq, residues, own_rows, proj_w):
        self.n, self.chips = n, n // CORES
        self.far = self.chips // 2
        self.seq, self.residues, self.rows, self.proj = seq, residues, own_rows, proj_w
        self.per = 16 // seq
        self.fold = LANES // proj_w
        self.chip_rows = CORES * own_rows
        self.left = proj_w * seq
        self.right = self.chip_rows // self.fold * seq
        self.pair = self.chip_rows * own_rows
        self.relayed = self.left + self.right

    def crosses(self, k):
        return k >= self.far and k % 2 == 0

    def right_at(self, k):
        return self.left + (self.right if self.crosses(k) else 0)

    def pair_at(self, k):
        return 0 if self.pair_only(k) else self.right_at(k) + self.right

    def pair_only(self, k):
        return k >= self.far and k % 2 == 1

    def total(self, k):
        return self.pair_at(k) + self.pair


def send_kernel(lay, place, x_ref, pair_ref, gain_ref, offset_ref, wl_ref, wr_ref, *rest):
    bufs, (left_ref, right_ref) = rest[: lay.chips], rest[lay.chips :]
    seq, residues, proj, fold = lay.seq, lay.residues, lay.proj, lay.fold
    f32, bf16 = jnp.float32, jnp.bfloat16
    nt = (((1,), (1,)), ((), ()))
    x = x_ref[...].reshape(seq * residues, x_ref.shape[2])
    normed = layer_norm(x, gain_ref[...], offset_ref[...]).astype(bf16)
    left = lax.dot_general(wl_ref[...], normed, nt, preferred_element_type=f32)
    for s in range(seq):
        left_ref[s * proj : (s + 1) * proj, :] = left[:, s * residues : (s + 1) * residues]
    for tile in range(proj // lay.per):
        rows = jnp.concatenate(
            [left_ref[pl.ds(tile * lay.per + b, seq, stride=proj), :] for b in range(lay.per)], axis=0
        ).astype(bf16)
        for k, buf in enumerate(bufs):
            if not lay.pair_only(k):
                buf[tile * 16 : (tile + 1) * 16, :] = rows
    groups = residues // fold
    wide = jnp.concatenate([wr_ref[...]] * fold, axis=0)
    right = lax.dot_general(normed, wide, nt, preferred_element_type=f32)
    row = lax.broadcasted_iota(jnp.int32, (residues, LANES), 0)
    lane = lax.broadcasted_iota(jnp.int32, (residues, LANES), 1)
    keep = lax.rem(row, fold) == lax.div(lane, proj)
    row = lax.broadcasted_iota(jnp.int32, (groups, residues), 0)
    lane = lax.broadcasted_iota(jnp.int32, (groups, residues), 1)
    stack = jnp.where(lax.div(lane, fold) == row, 1.0, 0.0).astype(bf16)
    for s in range(seq):
        own = jnp.where(keep, right[s * residues : (s + 1) * residues], 0.0).astype(bf16)
        right_ref[s * groups : (s + 1) * groups, :] = jnp.dot(stack, own, preferred_element_type=f32)

    def right_of(k):
        at = lax.bitwise_xor(place[0], k) * (lay.right // seq)
        rows = [right_ref[pl.ds(at + u, seq, stride=groups), :] for u in range(lay.right // seq)]
        return jnp.concatenate(rows, axis=0).astype(bf16)

    for k, buf in enumerate(bufs):
        if not lay.pair_only(k):
            at = lay.right_at(k)
            buf[at : at + lay.right, :] = right_of(k)
        if lay.crosses(k):
            buf[lay.left : lay.left + lay.right, :] = right_of(k ^ 1)
        at = pl.multiple_of(lax.bitwise_xor(place[0], k) * lay.chip_rows, lay.chip_rows)
        tile = pair_ref[:, pl.ds(at, lay.chip_rows), :].astype(f32)
        tile = jnp.swapaxes(tile, 0, 1).reshape(lay.pair, LANES)
        at = lay.pair_at(k)
        buf[at : at + lay.pair, :] = tile.astype(bf16)


def update_kernel(lay, outers, pairs, place, *rest):
    count = max([b for b, _ in outers] + [b for b, _, _ in pairs]) + 1
    bufs = rest[:count]
    (ow_ref, ob_ref, pg_ref, ps_ref, uw_ref, ub_ref, dw_ref, db_ref, out_ref, outer_ref, pair_ref) = rest[count:]
    seq, residues, proj, rows_j, fold, per = lay.seq, lay.residues, lay.proj, lay.rows, lay.fold, lay.per
    f32, bf16 = jnp.float32, jnp.bfloat16
    chip, core = place[0], place[1]
    groups = rows_j // fold
    own = pl.multiple_of(core * (groups * seq), groups * seq)
    spread = []
    for b in range(per):
        rows = []
        for m, at in outers:
            got = bufs[m][pl.ds(at + own, groups * seq), :].astype(f32)
            got = jnp.concatenate([got[u * seq : (u + 1) * seq] for u in range(groups)], axis=1)
            zero = jnp.zeros_like(got)
            rows += [got if h == b else zero for h in range(per)]
        spread.append(jnp.concatenate(rows, axis=0).T.astype(bf16))
    right = jnp.concatenate(spread, axis=0)
    wide = 4
    scale = 1.0 / (seq * lay.n)
    for tile in range(0, proj // per, wide):
        left = jnp.concatenate(
            [
                jnp.concatenate([bufs[m][t * 16 : (t + 1) * 16, :] for m, _ in outers], axis=0)
                for t in range(tile, tile + wide)
            ],
            axis=1,
        )
        x = (jnp.dot(right, left, preferred_element_type=f32) * scale).astype(bf16)
        for b in range(per):
            for w in range(wide):
                c = (tile + w) * per + b
                for j in range(rows_j):
                    at = (b * rows_j + j) * proj
                    outer_ref[c * proj : (c + 1) * proj, j * residues : (j + 1) * residues] = x[
                        at : at + proj, w * residues : (w + 1) * residues
                    ]
    own = pl.multiple_of(core * (rows_j * rows_j), rows_j * rows_j)
    for m, at, k in pairs:
        sender = lax.bitwise_xor(chip * CORES + core, k)
        got = bufs[m][pl.ds(at + own, rows_j * rows_j), :].astype(f32)
        for j in range(rows_j):
            pair_ref[j, pl.ds(pl.multiple_of(sender * rows_j, rows_j), rows_j), :] = got[j * rows_j : (j + 1) * rows_j]
    added = lax.dot_general(ow_ref[...], outer_ref[...], (((0,), (0,)), ((), ())), preferred_element_type=f32)
    step = 4
    for j0 in range(0, rows_j, step):
        summed = jnp.concatenate(
            [added[:, j * residues : (j + 1) * residues].T + pair_ref[j] for j in range(j0, j0 + step)], axis=0
        )
        summed = summed + ob_ref[...]
        normed = layer_norm(summed, pg_ref[...], ps_ref[...]).astype(bf16)
        hidden = jnp.dot(normed, uw_ref[...], preferred_element_type=f32) + ub_ref[...]
        hidden = jnp.maximum(hidden, 0.0).astype(bf16)
        result = summed + jnp.dot(hidden, dw_ref[...], preferred_element_type=f32) + db_ref[...]
        out_ref[j0 : j0 + step] = result.astype(bf16).reshape(step, residues, LANES)


MIB = 1 << 20


def in_hbm(x):
    return pltpu.with_memory_space_constraint(x, pltpu.HBM)


def in_vmem(x):
    return pltpu.with_memory_space_constraint(x, pltpu.VMEM)


def load_kernel(*refs):
    count = len(refs) // 2
    for source, to in zip(refs[:count], refs[count:]):
        to[...] = source[...]


def load(arrays):
    return pl.pallas_call(
        load_kernel,
        out_shape=[jax.ShapeDtypeStruct(a.shape, a.dtype) for a in arrays],
        in_specs=[VMEM] * len(arrays),
        out_specs=[VMEM] * len(arrays),
        compiler_params=pltpu.CompilerParams(vmem_limit_bytes=4 * MIB),
        name="load",
    )(*[in_hbm(a) for a in arrays])


def fast_shards(n, alignment, pair_rep, align_gain, align_offset, left_weight, right_weight, *layer_params):
    seq, residues, _ = alignment.shape
    lay = Layout(n, seq, residues, pair_rep.shape[0], left_weight.shape[1])
    f32, bf16 = jnp.float32, jnp.bfloat16
    me = lax.axis_index("row")
    place = jnp.stack([me // CORES, me % CORES]).astype(jnp.int32)
    sent = pl.pallas_call(
        functools.partial(send_kernel, lay),
        out_shape=[jax.ShapeDtypeStruct((lay.total(k), LANES), bf16) for k in range(lay.chips)],
        in_specs=[SMEM] + [VMEM] * 6,
        out_specs=[VMEM] * lay.chips,
        scratch_shapes=[
            pltpu.VMEM((seq * lay.proj, LANES), f32),
            pltpu.VMEM((seq * (residues // lay.fold), LANES), f32),
        ],
        compiler_params=pltpu.CompilerParams(vmem_limit_bytes=8 * MIB),
        name="send",
    )(
        place,
        in_hbm(alignment),
        in_hbm(pair_rep),
        in_hbm(align_gain.reshape(1, -1)),
        in_hbm(align_offset.reshape(1, -1)),
        in_hbm(left_weight.T),
        in_hbm(right_weight.T),
    )

    def permute(x, k):
        return lax.ppermute(x, "row", [(d, d ^ k) for d in range(n)])

    got = {k: permute(sent[k], CORES * k) if k else sent[0] for k in range(lay.chips)}
    relayed = {k: permute(got[k ^ 1][: lay.relayed], CORES) for k in range(lay.chips) if lay.pair_only(k)}
    operands, outers, pairs = [], [], []

    def take(x, k, core, outer, pair):
        if outer is not None:
            outers.append((len(operands), outer))
        if pair is not None:
            pairs.append((len(operands), pair, CORES * k + core))
        operands.append(x)

    for k in range(lay.chips):
        outer = None if lay.pair_only(k) else lay.right_at(k)
        take(got[k], k, 0, outer, lay.pair_at(k))
        take(permute(got[k], 1), k, 1, outer, lay.pair_at(k))
        if k in relayed:
            take(relayed[k], k, 0, lay.left, None)
            take(permute(relayed[k], 1), k, 1, lay.left, None)
    params = load([p if p.ndim == 2 else p.reshape(1, -1) for p in layer_params])
    rows_j = lay.rows
    return pl.pallas_call(
        functools.partial(update_kernel, lay, outers, pairs),
        out_shape=jax.ShapeDtypeStruct((rows_j, residues, LANES), bf16),
        in_specs=[SMEM] + [VMEM] * (len(operands) + 8),
        out_specs=VMEM,
        scratch_shapes=[
            pltpu.VMEM((lay.proj * lay.proj, rows_j * residues), bf16),
            pltpu.VMEM((rows_j, residues, LANES), f32),
        ],
        compiler_params=pltpu.CompilerParams(vmem_limit_bytes=16 * MIB),
        name="update",
    )(
        place,
        *[in_vmem(x) for x in operands],
        *[in_vmem(x) for x in params],
    )


def fits(n, alignment, pair_rep, left_weight):
    seq, residues, _ = alignment.shape
    rows, _, width = pair_rep.shape
    return (
        n >= 8
        and n & (n - 1) == 0
        and seq == 8
        and rows == 8
        and residues == LANES
        and width == LANES
        and left_weight.shape[1] == 32
    )


def solution(mesh):
    n = mesh.shape["row"]

    def shards(alignment, pair_rep, align_gain, align_offset, left_weight, right_weight, *layer_params):
        if fits(n, alignment, pair_rep, left_weight):
            return fast_shards(n, alignment, pair_rep, align_gain, align_offset, left_weight, right_weight, *layer_params)
        return plain_shards(alignment, pair_rep, align_gain, align_offset, left_weight, right_weight, *layer_params)

    split = P(("group", "row"), None, None)
    return jax.shard_map(
        shards,
        mesh=mesh,
        in_specs=(split, split) + (P(),) * 12,
        out_specs=split,
        check_vma=False,
    )
```
